32 devices in a mesh: groups: 2 (over y), tm: 16 (over z, x, core).
Axes of the slice: x: 2, y: 2, z: 4, core: 2. Of those that a mesh axis runs over, the one named last changes fastest.
Arguments:
- positions: float32 [128, 3, 1536], P(('groups', 'tm')), parts along dimension 0, may hold values from -6 to 6
- atom_pairs: int32 [2, 8192], replicated, may hold values from 0 to 1535, as said below
- frame_counts: int32 [32], P('groups'), parts along dimension 0, may hold values from 1 to 4, as said below
Outputs:
- mean_now: float32 [16384], P('groups'), parts along dimension 0
- mean_lag: float32 [16384], P('groups'), parts along dimension 0
- cov_now: float32 [16384, 8192], P(('groups', 'tm')), parts along dimension 0
- cov_lag: float32 [16384, 8192], P(('groups', 'tm')), parts along dimension 0
The draws below stay inside these ranges and needn't reach their ends.
There are 2 independent parts, one for each index of `groups`. The reference program is written for one: setup_inputs(seed, part) draws one part's arguments, and reference() takes and returns one part's arrays. A program takes and returns all parts, laid end to end along the dimension named above; an argument that names none is the same for every part. Nothing has to cross between parts.
Inputs may be any that keep to these rules, and one draw needn't show every extreme that they name: `atom_pairs`: the two atoms of a pair differ; every atom is the first atom of some pair. Each block's valid frames are its first frame_counts frames; in every draw one block holds 4 valid frames and another 1.
All inputs are finite; a program needn't handle non-finite values.
Results may differ from the reference program's by a relative error of at most 0.0029.
Values sent between devices are 32-bit elements; how exact they have to be, the bound alone decides.
A program may use at most 192 MiB of HBM per device.

```python
import jax
import jax.numpy as jnp
from jax import lax

PAIRS = 8192
ATOMS = 1536
FR = 4
LAG = 1
BLOCKS = 16
TOTAL = 64


def draw_positions(key, part):
    keys = jax.random.split(key, 5)
    frame_index = jnp.arange(TOTAL, dtype=jnp.float32)[:, None, None]
    base = 1.5 * jax.random.truncated_normal(keys[0], -3.0, 3.0, (1, 3, ATOMS), jnp.float32)
    period = jnp.exp(jax.random.uniform(keys[1], (1, 3, ATOMS), jnp.float32, minval=jnp.log(4.0 * LAG), maxval=jnp.log(4.0 * TOTAL)))
    phase = jax.random.uniform(keys[2], (1, 3, ATOMS), jnp.float32, minval=-3.14159, maxval=3.14159)
    amplitude = jax.random.uniform(keys[3], (1, 3, ATOMS), jnp.float32, minval=0.2, maxval=0.6)
    noise = 0.15 * jax.random.truncated_normal(keys[4], -3.0, 3.0, (TOTAL, 3, ATOMS), jnp.float32)
    wave = jnp.sin(6.2831853 * frame_index / period + phase)
    return (base + amplitude * wave + noise).astype(jnp.float32)


def draw_atom_pairs(key, part):
    keys = jax.random.split(key, 2)
    ordering = jax.random.permutation(keys[0], ATOMS).astype(jnp.int32)
    first_atom = ordering[jnp.arange(PAIRS, dtype=jnp.int32) % ATOMS]
    offsets = jax.random.randint(keys[1], (PAIRS,), 1, ATOMS, dtype=jnp.int32)
    second_atom = (first_atom + offsets) % ATOMS
    return jnp.stack([first_atom, second_atom]).astype(jnp.int32)


def draw_frame_counts(key, part):
    keys = jax.random.split(key, 3)
    lowest = FR // 4
    counts = jax.random.randint(keys[0], (BLOCKS,), lowest, FR + 1, dtype=jnp.int32)
    full_block = jax.random.randint(keys[1], (), 0, BLOCKS, dtype=jnp.int32)
    short_block = (full_block + jax.random.randint(keys[2], (), 1, BLOCKS, dtype=jnp.int32)) % BLOCKS
    counts = counts.at[full_block].set(FR)
    counts = counts.at[short_block].set(lowest)
    return counts.astype(jnp.int32)


def setup_inputs(seed: int = 0, part: int = 0) -> dict:
    key_of = jax.random.split(jax.random.key(seed), 4)
    own_keys = jax.random.split(jax.random.fold_in(key_of[3], part), 4)
    positions = draw_positions(jax.random.fold_in(jax.random.fold_in(key_of[3], part), 71), part)
    atom_pairs = draw_atom_pairs(jax.random.fold_in(key_of[3], 71), part)
    frame_counts = draw_frame_counts(jax.random.fold_in(jax.random.fold_in(key_of[3], part), 71), part)
    return dict(positions=positions, atom_pairs=atom_pairs, frame_counts=frame_counts)


def featurize(frames, atom_pairs):
    first_atom = jnp.take(frames, atom_pairs[0], axis=2)
    second_atom = jnp.take(frames, atom_pairs[1], axis=2)
    difference = first_atom - second_atom
    return jnp.sqrt(lax.optimization_barrier(jnp.sum(difference * difference, axis=1)))

def reference(positions, atom_pairs, frame_counts):
    total = positions.shape[0]
    frame_index = jnp.arange(total, dtype=jnp.int32)
    block_of = (frame_index // FR).astype(jnp.int32)
    valid = frame_index % FR < frame_counts[block_of]
    valid_ahead = jnp.concatenate([valid[LAG:], jnp.zeros((LAG,), dtype=bool)])
    weights = (valid & valid_ahead).astype(jnp.float32)
    pair_count = jnp.sum(weights)
    features = featurize(positions, atom_pairs)
    ahead = jnp.concatenate([features[LAG:], jnp.zeros((LAG, features.shape[1]), jnp.float32)], axis=0)
    mean_now = lax.optimization_barrier(jnp.sum(weights[:, None] * features, axis=0)) / pair_count
    mean_lag = lax.optimization_barrier(jnp.sum(weights[:, None] * ahead, axis=0)) / pair_count
    early = lax.optimization_barrier((features - mean_now).astype(jnp.bfloat16)).astype(jnp.float32)
    late = lax.optimization_barrier((ahead - mean_lag).astype(jnp.bfloat16)).astype(jnp.float32)
    weighted = early * weights[:, None]
    cov_now = jnp.dot(weighted.T, early, preferred_element_type=jnp.float32, precision=lax.Precision.HIGHEST) / pair_count
    cov_lag = jnp.dot(weighted.T, late, preferred_element_type=jnp.float32, precision=lax.Precision.HIGHEST) / pair_count
    return (mean_now, mean_lag, cov_now, cov_lag)
```

```python
import functools

import jax
import jax.numpy as jnp
from jax import lax
from jax.experimental import pallas as pl
from jax.experimental.pallas import tpu as pltpu
from jax.sharding import PartitionSpec as P

FR = 4
LAG = 1


def axis_split(devices):
    cores = 2 if devices % 2 == 0 else 1
    chips = devices // cores
    x = 1
    while x * x * x * 8 <= chips and chips % (x * 2) == 0:
        x *= 2
    return chips // x, x, cores


def gather_kernel(sizes, own_ref, all_ref, local_sem, send_sem, recv_sem):
    zs, xs, cs = sizes
    me = lax.axis_index("tm")
    core = lax.rem(me, cs)
    x = lax.rem(me // cs, xs)
    z = me // (cs * xs)

    def index(zi, xi, ci):
        return (zi * xs + xi) * cs + ci

    z_peers = [lax.rem(z + d, zs) for d in range(1, zs)]
    x_peers = [lax.rem(x + d, xs) for d in range(1, xs)]
    c_peers = [lax.rem(core + d, cs) for d in range(1, cs)]
    targets = (
        [index(p, x, core) for p in z_peers]
        + [index(z, p, core) for p in x_peers]
        + [index(z, x, p) for p in c_peers]
    )
    barrier = pltpu.get_barrier_semaphore()
    for target in targets:
        pl.semaphore_signal(
            barrier, inc=1, device_id={"tm": target}, device_id_type=pl.DeviceIdType.MESH
        )
    pl.semaphore_wait(barrier, len(targets))

    sent = []

    def send(source, block, target):
        copy = pltpu.make_async_remote_copy(
            src_ref=source,
            dst_ref=all_ref.at[block],
            send_sem=send_sem.at[len(sent)],
            recv_sem=recv_sem.at[block],
            device_id={"tm": target},
            device_id_type=pl.DeviceIdType.MESH,
        )
        copy.start()
        sent.append(copy)

    def arrived(block):
        pltpu.make_async_remote_copy(
            src_ref=all_ref.at[block],
            dst_ref=all_ref.at[block],
            send_sem=send_sem.at[0],
            recv_sem=recv_sem.at[block],
            device_id={"tm": me},
            device_id_type=pl.DeviceIdType.MESH,
        ).wait_recv()

    for p in z_peers:
        send(own_ref, me, index(p, x, core))
    for p in x_peers:
        send(own_ref, me, index(z, p, core))
    for p in c_peers:
        send(own_ref, me, index(z, x, p))
    local = pltpu.make_async_copy(own_ref, all_ref.at[me], local_sem)
    local.start()
    for zi in z_peers:
        block = index(zi, x, core)
        arrived(block)
        for p in x_peers:
            send(all_ref.at[block], block, index(z, p, core))
        for p in c_peers:
            send(all_ref.at[block], block, index(z, x, p))
    for zi in [z] + z_peers:
        for xi in x_peers:
            block = index(zi, xi, core)
            arrived(block)
            for p in c_peers:
                send(all_ref.at[block], block, index(z, x, p))
    for zi in [z] + z_peers:
        for xi in [x] + x_peers:
            for ci in c_peers:
                arrived(index(zi, xi, ci))
    local.wait()
    for copy in sent:
        copy.wait_send()


def gather_blocks(block, devices):
    sizes = axis_split(devices)
    zs, xs, cs = sizes
    sends = (zs - 1) + zs * (xs - 1) + zs * xs * (cs - 1)
    return pl.pallas_call(
        functools.partial(gather_kernel, sizes),
        out_shape=jax.ShapeDtypeStruct((devices,) + block.shape, block.dtype),
        in_specs=[pl.BlockSpec(memory_space=pl.ANY)],
        out_specs=pl.BlockSpec(memory_space=pl.ANY),
        scratch_shapes=[
            pltpu.SemaphoreType.DMA,
            pltpu.SemaphoreType.DMA((max(sends, 1),)),
            pltpu.SemaphoreType.DMA((devices,)),
        ],
        compiler_params=pltpu.CompilerParams(collective_id=0, has_side_effects=True),
        name="gather_positions",
    )(block)


def shifted_up(rows):
    return jnp.concatenate([rows[LAG:], jnp.zeros((LAG, rows.shape[1]), rows.dtype)], axis=0)


def covariance_kernel(
    frames,
    row_count,
    counts_ref,
    positions_ref,
    pairs_ref,
    mean_now_ref,
    mean_lag_ref,
    cov_now_ref,
    cov_lag_ref,
    split_ref,
    weights_ref,
    left_ref,
):
    step = pl.program_id(0)
    chunk = cov_now_ref.shape[1]
    atoms = positions_ref.shape[3]

    def features_of(start, width):
        atom = lax.broadcasted_iota(jnp.int32, (atoms, width), 0)
        first = pairs_ref[0:1, pl.ds(start, width)]
        second = pairs_ref[1:2, pl.ds(start, width)]
        select = jnp.where(atom == first, 1.0, jnp.where(atom == second, -1.0, 0.0)).astype(
            jnp.bfloat16
        )
        parts = jnp.dot(split_ref[...], select, preferred_element_type=jnp.float32)
        rows = 3 * frames
        difference = parts[:rows] + (parts[rows : 2 * rows] + parts[2 * rows :])
        squares = difference * difference
        return jnp.sqrt(
            squares[:frames] + squares[frames : 2 * frames] + squares[2 * frames :]
        )

    def scale():
        return 1.0 / jnp.sum(weights_ref[...], axis=0, keepdims=True)

    def widened(row, width):
        return jnp.concatenate([row] * (width // 128), axis=1)

    def means_of(features, ahead):
        width = features.shape[1]
        weights = widened(weights_ref[...], width)
        pair_count = jnp.sum(weights, axis=0, keepdims=True)
        mean_now = jnp.sum(weights * features, axis=0, keepdims=True) / pair_count
        mean_lag = jnp.sum(weights * ahead, axis=0, keepdims=True) / pair_count
        return mean_now, mean_lag

    @pl.when(step == 0)
    def _():
        for c in range(3):
            values = positions_ref[:, c, :, :].reshape(frames, atoms)
            high = values.astype(jnp.bfloat16)
            rest = values - high.astype(jnp.float32)
            middle = rest.astype(jnp.bfloat16)
            low = (rest - middle.astype(jnp.float32)).astype(jnp.bfloat16)
            for s, part in enumerate((high, middle, low)):
                split_ref[pl.ds((3 * s + c) * frames, frames), :] = part
        frame = lax.broadcasted_iota(jnp.int32, (frames, 128), 0)

        def add_block(b, current):
            return jnp.where(frame // FR == b, counts_ref[b], current)

        current = lax.fori_loop(0, frames // FR, add_block, jnp.zeros((frames, 128), jnp.int32))
        valid = jnp.where(frame % FR < current, 1.0, 0.0)
        weights_ref[...] = valid * shifted_up(valid)

        own_width = max(row_count, 128)
        own_start = lax.axis_index("tm") * row_count
        base = pl.multiple_of(own_start // own_width * own_width, own_width)
        features = features_of(base, own_width)
        mean_now, _unused = means_of(features, shifted_up(features))
        early = (features - mean_now).astype(jnp.bfloat16).astype(jnp.float32)
        left = early * widened(weights_ref[...], own_width)
        left_ref[...] = jnp.transpose(left).astype(jnp.bfloat16)

    features = features_of(pl.multiple_of(step * chunk, chunk), chunk)
    ahead = shifted_up(features)
    mean_now, mean_lag = means_of(features, ahead)
    mean_now_ref[...] = mean_now
    mean_lag_ref[...] = mean_lag
    early = (features - mean_now).astype(jnp.bfloat16)
    late = (ahead - mean_lag).astype(jnp.bfloat16)
    if row_count == left_ref.shape[0]:
        left = left_ref[...]
    else:
        offset = lax.rem(lax.axis_index("tm") * row_count, left_ref.shape[0])
        left = left_ref[pl.ds(pl.multiple_of(offset, row_count), row_count), :]
    factor = widened(scale(), chunk)
    cov_now_ref[...] = jnp.dot(left, early, preferred_element_type=jnp.float32) * factor
    cov_lag_ref[...] = jnp.dot(left, late, preferred_element_type=jnp.float32) * factor


def covariances(positions, atom_pairs, frame_counts, row_count):
    devices, _, block_frames, atoms = positions.shape
    frames = devices * block_frames
    width = atom_pairs.shape[1]
    chunk = 512 if frames <= 128 else 128
    row = jax.ShapeDtypeStruct((1, width), jnp.float32)
    matrix = jax.ShapeDtypeStruct((row_count, width), jnp.float32)
    return pl.pallas_call(
        functools.partial(covariance_kernel, frames, row_count),
        out_shape=(row, row, matrix, matrix),
        grid=(width // chunk,),
        in_specs=[
            pl.BlockSpec(memory_space=pltpu.SMEM),
            pl.BlockSpec(positions.shape, lambda i: (0, 0, 0, 0), pipeline_mode=pl.Buffered(1)),
            pl.BlockSpec((2, width), lambda i: (0, 0), pipeline_mode=pl.Buffered(1)),
        ],
        out_specs=(
            pl.BlockSpec((1, chunk), lambda i: (0, i)),
            pl.BlockSpec((1, chunk), lambda i: (0, i)),
            pl.BlockSpec((row_count, chunk), lambda i: (0, i)),
            pl.BlockSpec((row_count, chunk), lambda i: (0, i)),
        ),
        scratch_shapes=[
            pltpu.VMEM((9 * frames, atoms), jnp.bfloat16),
            pltpu.VMEM((frames, 128), jnp.float32),
            pltpu.VMEM((max(row_count, 128), frames), jnp.bfloat16),
        ],
        compiler_params=pltpu.CompilerParams(vmem_limit_bytes=60 * 1024 * 1024),
        name="covariances",
    )(frame_counts, positions, atom_pairs)


def body(positions, atom_pairs, frame_counts):
    devices = lax.axis_size("tm")
    width = atom_pairs.shape[1]
    gathered = gather_blocks(jnp.transpose(positions, (1, 0, 2)), devices)
    mean_now, mean_lag, cov_now, cov_lag = covariances(
        gathered, atom_pairs, frame_counts, width // devices
    )
    return (mean_now.reshape(width), mean_lag.reshape(width), cov_now, cov_lag)


def solution(mesh):
    return jax.shard_map(
        body,
        mesh=mesh,
        in_specs=(P(("groups", "tm"), None, None), P(), P("groups")),
        out_specs=(P("groups"), P("groups"), P(("groups", "tm"), None), P(("groups", "tm"), None)),
        check_vma=False,
    )
```

```python
import functools

import jax
import jax.numpy as jnp
from jax import lax
from jax.experimental import pallas as pl
from jax.experimental.pallas import tpu as pltpu
from jax.sharding import PartitionSpec as P

FR = 4
LAG = 1
CORES = 2


def axis_split(devices):
    chips = devices // CORES
    x = 1
    while x * x * x * 8 <= chips and chips % (x * 2) == 0:
        x *= 2
    return chips // x, x


def features_kernel(
    sizes,
    own_ref,
    pairs_ref,
    features_ref,
    blocks_ref,
    select_ref,
    split_ref,
    result_ref,
    local_sem,
    send_sem,
    recv_sem,
    keep_sem,
    share_sem,
    fetch_sem,
):
    zs, xs = sizes
    me = lax.axis_index("tm")
    core = lax.rem(me, CORES)
    x = lax.rem(me // CORES, xs)
    z = me // (CORES * xs)
    chunks, atoms, width = select_ref.shape
    frames = blocks_ref.shape[0] * FR

    def device(zi, xi, ci):
        return {"tm": (zi * xs + xi) * CORES + ci}

    sibling = device(z, x, 1 - core)
    above = z + 1 < zs
    below = z > 0
    x_peers = [lax.rem(x + d, xs) for d in range(1, xs)]

    barrier = pltpu.get_barrier_semaphore()

    def greet(target):
        pl.semaphore_signal(
            barrier, inc=1, device_id=target, device_id_type=pl.DeviceIdType.MESH
        )

    @pl.when(above)
    def _():
        greet(device(z + 1, x, core))

    @pl.when(below)
    def _():
        greet(device(z - 1, x, core))

    for p in x_peers:
        greet(device(z, p, core))
    greet(sibling)
    local = pltpu.make_async_copy(own_ref, blocks_ref.at[z * xs + x], local_sem)
    local.start()
    met = above.astype(jnp.int32) + below.astype(jnp.int32) + len(x_peers) + 1
    pl.semaphore_wait(barrier, met)

    sent = []

    def send(source, block, target, allowed):
        copy = pltpu.make_async_remote_copy(
            src_ref=source,
            dst_ref=blocks_ref.at[block],
            send_sem=send_sem.at[len(sent)],
            recv_sem=recv_sem.at[block],
            device_id=target,
            device_id_type=pl.DeviceIdType.MESH,
        )
        sent.append((copy, allowed))
        if allowed is None:
            copy.start()
        else:
            pl.when(allowed)(copy.start)

    def arrived(block):
        pltpu.make_async_remote_copy(
            src_ref=blocks_ref.at[block],
            dst_ref=blocks_ref.at[block],
            send_sem=send_sem.at[0],
            recv_sem=recv_sem.at[block],
            device_id=sibling,
            device_id_type=pl.DeviceIdType.MESH,
        ).wait_recv()

    def build_select(j, carry):
        atom = lax.broadcasted_iota(jnp.int32, (atoms, width), 0)
        start = pl.multiple_of(j * width, width)
        first = pairs_ref[0:1, pl.ds(start, width)]
        second = pairs_ref[1:2, pl.ds(start, width)]
        select_ref[j] = jnp.where(
            atom == first, 1.0, jnp.where(atom == second, -1.0, 0.0)
        ).astype(jnp.bfloat16)
        return carry

    built = [chunks * d // zs for d in range(zs + 1)]

    def build_some(d):
        lax.fori_loop(built[d], built[d + 1], build_select, 0)

    mine = z * xs + x
    send(own_ref, mine, device(z + 1, x, core), above)
    send(own_ref, mine, device(z - 1, x, core), below)
    for p in x_peers:
        send(own_ref, mine, device(z, p, core), None)
    for d in range(1, zs):
        build_some(d - 1)
        for sign in (-1, 1):
            origin = z + sign * d
            exists = origin >= 0 if sign < 0 else origin < zs
            block = origin * xs + x
            pl.when(exists)(functools.partial(arrived, block))
            if d < zs - 1:
                onward = above if sign < 0 else below
                send(
                    blocks_ref.at[block],
                    block,
                    device(z - sign, x, core),
                    jnp.logical_and(exists, onward),
                )
            for p in x_peers:
                send(blocks_ref.at[block], block, device(z, p, core), exists)
    build_some(zs - 1)
    for zi in range(zs):
        for p in x_peers:
            arrived(zi * xs + p)
    local.wait()

    for c in range(3):
        values = blocks_ref[:, c, :, :].reshape(frames, atoms)
        high = values.astype(jnp.bfloat16)
        rest = values - high.astype(jnp.float32)
        middle = rest.astype(jnp.bfloat16)
        low = (rest - middle.astype(jnp.float32)).astype(jnp.bfloat16)
        for s, part in enumerate((high, middle, low)):
            split_ref[pl.ds((3 * s + c) * frames, frames), :] = part

    def keep(j):
        return pltpu.make_async_copy(
            result_ref.at[j], features_ref.at[core, j], keep_sem.at[j]
        )

    def share(j):
        return pltpu.make_async_remote_copy(
            src_ref=result_ref.at[j],
            dst_ref=features_ref.at[core, j],
            send_sem=share_sem.at[j],
            recv_sem=fetch_sem.at[j],
            device_id=sibling,
            device_id_type=pl.DeviceIdType.MESH,
        )

    def publish(j):
        keep(j).start()
        share(j).start()

    def featurize(j):
        parts = jnp.dot(split_ref[...], select_ref[j], preferred_element_type=jnp.float32)
        rows = 3 * frames
        difference = parts[:rows] + (parts[rows : 2 * rows] + parts[2 * rows :])
        squares = difference * difference
        result_ref[j] = jnp.sqrt(
            squares[:frames] + squares[frames : 2 * frames] + squares[2 * frames :]
        )

    def step(j, carry):
        featurize(j)
        publish(j - 1)
        return carry

    featurize(0)
    lax.fori_loop(1, chunks, step, 0)
    publish(chunks - 1)

    def finish(j, carry):
        keep(j).wait()
        share(j).wait_send()
        share(j).wait_recv()
        return carry

    lax.fori_loop(0, chunks, finish, 0)
    for copy, allowed in sent:
        if allowed is None:
            copy.wait_send()
        else:
            pl.when(allowed)(copy.wait_send)


def shared_features(block, atom_pairs, devices, chunk):
    zs, xs = axis_split(devices)
    held = devices // CORES
    frames = held * FR
    atoms = block.shape[2]
    chunks = atom_pairs.shape[1] // chunk
    sends = 2 + (xs - 1) + 2 * (zs - 1) * xs
    dma = pltpu.SemaphoreType.DMA
    return pl.pallas_call(
        functools.partial(features_kernel, (zs, xs)),
        out_shape=jax.ShapeDtypeStruct((CORES, chunks, frames, chunk), jnp.float32),
        in_specs=[
            pl.BlockSpec(memory_space=pl.ANY),
            pl.BlockSpec(memory_space=pltpu.VMEM),
        ],
        out_specs=pl.BlockSpec(memory_space=pl.ANY),
        scratch_shapes=[
            pltpu.VMEM((held,) + block.shape, jnp.float32),
            pltpu.VMEM((chunks, atoms, chunk), jnp.bfloat16),
            pltpu.VMEM((9 * frames, atoms), jnp.bfloat16),
            pltpu.VMEM((chunks, frames, chunk), jnp.float32),
            dma,
            dma((sends,)),
            dma((held,)),
            dma((chunks,)),
            dma((chunks,)),
            dma((chunks,)),
        ],
        compiler_params=pltpu.CompilerParams(
            collective_id=0, has_side_effects=True, vmem_limit_bytes=60 * 1024 * 1024
        ),
        name="features",
    )(block, atom_pairs)


def moved(rows, by):
    zeros = jnp.zeros((abs(by), rows.shape[1]), rows.dtype)
    if by > 0:
        return jnp.concatenate([rows[by:], zeros], axis=0)
    return jnp.concatenate([zeros, rows[:by]], axis=0)


def next_frames(even, odd):
    last = lax.broadcasted_iota(jnp.int32, even.shape, 0) % FR == FR - LAG
    up = moved(even, 1)
    ahead_even = jnp.where(last, moved(odd, 1 - FR), up)
    ahead_odd = jnp.where(last, up, moved(odd, 1))
    return jnp.concatenate([ahead_even, ahead_odd], axis=0)


def covariance_kernel(
    row_count,
    counts_ref,
    features_ref,
    mean_now_ref,
    mean_lag_ref,
    cov_now_ref,
    cov_lag_ref,
    weights_ref,
    left_ref,
):
    step = pl.program_id(0)
    _, _, frames, width = features_ref.shape

    def widened(rows):
        return jnp.concatenate([rows] * (width // 128), axis=1)

    def frames_of(j):
        even = features_ref[0, j]
        odd = features_ref[1, j]
        return jnp.concatenate([even, odd], axis=0), next_frames(even, odd)

    def pair_count():
        return jnp.sum(weights_ref[...], axis=0, keepdims=True)

    def mean_of(rows):
        total = jnp.sum(widened(weights_ref[...]) * rows, axis=0, keepdims=True)
        return total / widened(pair_count())

    @pl.when(step == 0)
    def _():
        frame = lax.broadcasted_iota(jnp.int32, (frames, 128), 0)

        def valid_of(core):
            def add_block(b, current):
                return jnp.where(frame // FR == b, counts_ref[CORES * b + core], current)

            current = lax.fori_loop(
                0, frames // FR, add_block, jnp.zeros((frames, 128), jnp.int32)
            )
            return jnp.where(frame % FR < current, 1.0, 0.0)

        even = valid_of(0)
        odd = valid_of(1)
        weights_ref[...] = jnp.concatenate([even, odd], axis=0) * next_frames(even, odd)
        start = lax.axis_index("tm") * row_count
        features, _unused = frames_of(start // width)
        early = (features - mean_of(features)).astype(jnp.bfloat16).astype(jnp.float32)
        left = early * widened(weights_ref[...])
        left_ref[...] = jnp.transpose(left).astype(jnp.bfloat16)

    features, ahead = frames_of(step)
    mean_now = mean_of(features)
    mean_lag = mean_of(ahead)
    mean_now_ref[...] = mean_now
    mean_lag_ref[...] = mean_lag
    early = (features - mean_now).astype(jnp.bfloat16)
    late = (ahead - mean_lag).astype(jnp.bfloat16)
    if row_count == width:
        left = left_ref[...]
    else:
        offset = lax.rem(lax.axis_index("tm") * row_count, width)
        left = left_ref[pl.ds(pl.multiple_of(offset, row_count), row_count), :]
    factor = widened(1.0 / pair_count())
    cov_now_ref[...] = jnp.dot(left, early, preferred_element_type=jnp.float32) * factor
    cov_lag_ref[...] = jnp.dot(left, late, preferred_element_type=jnp.float32) * factor


def covariances(features, frame_counts, row_count):
    _, chunks, frames, chunk = features.shape
    width = chunks * chunk
    row = jax.ShapeDtypeStruct((1, width), jnp.float32)
    matrix = jax.ShapeDtypeStruct((row_count, width), jnp.float32)
    return pl.pallas_call(
        functools.partial(covariance_kernel, row_count),
        out_shape=(row, row, matrix, matrix),
        grid=(chunks,),
        in_specs=[
            pl.BlockSpec(memory_space=pltpu.SMEM),
            pl.BlockSpec(
                features.shape, lambda i: (0, 0, 0, 0), pipeline_mode=pl.Buffered(1)
            ),
        ],
        out_specs=(
            pl.BlockSpec((1, chunk), lambda i: (0, i)),
            pl.BlockSpec((1, chunk), lambda i: (0, i)),
            pl.BlockSpec((row_count, chunk), lambda i: (0, i)),
            pl.BlockSpec((row_count, chunk), lambda i: (0, i)),
        ),
        scratch_shapes=[
            pltpu.VMEM((CORES * frames, 128), jnp.float32),
            pltpu.VMEM((chunk, CORES * frames), jnp.bfloat16),
        ],
        compiler_params=pltpu.CompilerParams(vmem_limit_bytes=60 * 1024 * 1024),
        name="covariances",
    )(frame_counts, features)


def body(positions, atom_pairs, frame_counts):
    devices = lax.axis_size("tm")
    width = atom_pairs.shape[1]
    row_count = width // devices
    chunk = 512 if devices <= 32 else 128
    features = shared_features(
        jnp.transpose(positions, (1, 0, 2)), atom_pairs, devices, chunk
    )
    mean_now, mean_lag, cov_now, cov_lag = covariances(features, frame_counts, row_count)
    return (mean_now.reshape(width), mean_lag.reshape(width), cov_now, cov_lag)


def solution(mesh):
    return jax.shard_map(
        body,
        mesh=mesh,
        in_specs=(P(("groups", "tm"), None, None), P(), P("groups")),
        out_specs=(P("groups"), P("groups"), P(("groups", "tm"), None), P(("groups", "tm"), None)),
        check_vma=False,
    )
```

```python
import functools

import jax
import jax.numpy as jnp
from jax import lax
from jax.experimental import pallas as pl
from jax.experimental.pallas import tpu as pltpu
from jax.sharding import PartitionSpec as P

FR = 4
LAG = 1
CORES = 2


def axis_split(devices):
    chips = devices // CORES
    x = 1
    while x * x * x * 8 <= chips and chips % (x * 2) == 0:
        x *= 2
    return chips // x, x


def features_kernel(
    sizes,
    own_ref,
    pairs_ref,
    features_ref,
    blocks_ref,
    select_ref,
    split_ref,
    result_ref,
    local_sem,
    send_sem,
    recv_sem,
    keep_sem,
    share_sem,
    fetch_sem,
):
    zs, xs = sizes
    me = lax.axis_index("tm")
    core = lax.rem(me, CORES)
    x = lax.rem(me // CORES, xs)
    z = me // (CORES * xs)
    chunks, atoms, width = select_ref.shape
    frames = blocks_ref.shape[0] * FR

    def device(zi, xi, ci):
        return {"tm": (zi * xs + xi) * CORES + ci}

    sibling = device(z, x, 1 - core)
    above = z + 1 < zs
    below = z > 0
    x_peers = [lax.rem(x + d, xs) for d in range(1, xs)]

    barrier = pltpu.get_barrier_semaphore()

    def greet(target):
        pl.semaphore_signal(
            barrier, inc=1, device_id=target, device_id_type=pl.DeviceIdType.MESH
        )

    @pl.when(above)
    def _():
        greet(device(z + 1, x, core))

    @pl.when(below)
    def _():
        greet(device(z - 1, x, core))

    for p in x_peers:
        greet(device(z, p, core))
    greet(sibling)
    local = pltpu.make_async_copy(own_ref, blocks_ref.at[z * xs + x], local_sem)
    local.start()
    met = above.astype(jnp.int32) + below.astype(jnp.int32) + len(x_peers) + 1
    pl.semaphore_wait(barrier, met)

    sent = []

    def send(source, block, target, allowed):
        copy = pltpu.make_async_remote_copy(
            src_ref=source,
            dst_ref=blocks_ref.at[block],
            send_sem=send_sem.at[len(sent)],
            recv_sem=recv_sem.at[block],
            device_id=target,
            device_id_type=pl.DeviceIdType.MESH,
        )
        sent.append((copy, allowed))
        if allowed is None:
            copy.start()
        else:
            pl.when(allowed)(copy.start)

    def arrived(block):
        pltpu.make_async_remote_copy(
            src_ref=blocks_ref.at[block],
            dst_ref=blocks_ref.at[block],
            send_sem=send_sem.at[0],
            recv_sem=recv_sem.at[block],
            device_id=sibling,
            device_id_type=pl.DeviceIdType.MESH,
        ).wait_recv()

    def build_select(j, carry):
        atom = lax.broadcasted_iota(jnp.int32, (atoms, width), 0).astype(jnp.int16)
        start = pl.multiple_of(j * width, width)
        first = pairs_ref[0:1, pl.ds(start, width)].astype(jnp.int16)
        second = pairs_ref[1:2, pl.ds(start, width)].astype(jnp.int16)
        one, zero = jnp.bfloat16(1.0), jnp.bfloat16(0.0)
        select_ref[j] = jnp.where(atom == first, one, jnp.where(atom == second, -one, zero))
        return carry

    built = [chunks * d // zs for d in range(zs + 1)]

    def build_some(d):
        lax.fori_loop(built[d], built[d + 1], build_select, 0)

    mine = z * xs + x
    send(own_ref, mine, device(z + 1, x, core), above)
    send(own_ref, mine, device(z - 1, x, core), below)
    for p in x_peers:
        send(own_ref, mine, device(z, p, core), None)
    for d in range(1, zs):
        build_some(d - 1)
        for sign in (-1, 1):
            origin = z + sign * d
            exists = origin >= 0 if sign < 0 else origin < zs
            block = origin * xs + x
            pl.when(exists)(functools.partial(arrived, block))
            if d < zs - 1:
                onward = above if sign < 0 else below
                send(
                    blocks_ref.at[block],
                    block,
                    device(z - sign, x, core),
                    jnp.logical_and(exists, onward),
                )
            for p in x_peers:
                send(blocks_ref.at[block], block, device(z, p, core), exists)
    build_some(zs - 1)
    for zi in range(zs):
        for p in x_peers:
            arrived(zi * xs + p)
    local.wait()

    for c in range(3):
        values = blocks_ref[:, c, :, :].reshape(frames, atoms)
        high = values.astype(jnp.bfloat16)
        rest = values - high.astype(jnp.float32)
        middle = rest.astype(jnp.bfloat16)
        low = (rest - middle.astype(jnp.float32)).astype(jnp.bfloat16)
        for s, part in enumerate((high, middle, low)):
            split_ref[pl.ds((3 * s + c) * frames, frames), :] = part

    def keep(j):
        return pltpu.make_async_copy(
            result_ref.at[j], features_ref.at[core, j], keep_sem.at[j]
        )

    def share(j):
        return pltpu.make_async_remote_copy(
            src_ref=result_ref.at[j],
            dst_ref=features_ref.at[core, j],
            send_sem=share_sem.at[j],
            recv_sem=fetch_sem.at[j],
            device_id=sibling,
            device_id_type=pl.DeviceIdType.MESH,
        )

    def publish(j):
        keep(j).start()
        share(j).start()

    def featurize(j):
        parts = jnp.dot(split_ref[...], select_ref[j], preferred_element_type=jnp.float32)
        rows = 3 * frames
        difference = parts[:rows] + (parts[rows : 2 * rows] + parts[2 * rows :])
        squares = difference * difference
        result_ref[j] = jnp.sqrt(
            squares[:frames] + squares[frames : 2 * frames] + squares[2 * frames :]
        )

    def step(j, carry):
        featurize(j)
        publish(j - 1)
        return carry

    featurize(0)
    lax.fori_loop(1, chunks, step, 0)
    publish(chunks - 1)

    def finish(j, carry):
        keep(j).wait()
        share(j).wait_send()
        share(j).wait_recv()
        return carry

    lax.fori_loop(0, chunks, finish, 0)
    for copy, allowed in sent:
        if allowed is None:
            copy.wait_send()
        else:
            pl.when(allowed)(copy.wait_send)


def shared_features(block, atom_pairs, devices, chunk):
    zs, xs = axis_split(devices)
    held = devices // CORES
    frames = held * FR
    atoms = block.shape[2]
    chunks = atom_pairs.shape[1] // chunk
    sends = 2 + (xs - 1) + 2 * (zs - 1) * xs
    dma = pltpu.SemaphoreType.DMA
    return pl.pallas_call(
        functools.partial(features_kernel, (zs, xs)),
        out_shape=jax.ShapeDtypeStruct((CORES, chunks, frames, chunk), jnp.float32),
        in_specs=[
            pl.BlockSpec(memory_space=pl.ANY),
            pl.BlockSpec(memory_space=pltpu.VMEM),
        ],
        out_specs=pl.BlockSpec(memory_space=pl.ANY),
        scratch_shapes=[
            pltpu.VMEM((held,) + block.shape, jnp.float32),
            pltpu.VMEM((chunks, atoms, chunk), jnp.bfloat16),
            pltpu.VMEM((9 * frames, atoms), jnp.bfloat16),
            pltpu.VMEM((chunks, frames, chunk), jnp.float32),
            dma,
            dma((sends,)),
            dma((held,)),
            dma((chunks,)),
            dma((chunks,)),
            dma((chunks,)),
        ],
        compiler_params=pltpu.CompilerParams(
            collective_id=0, has_side_effects=True, vmem_limit_bytes=60 * 1024 * 1024
        ),
        name="features",
    )(block, atom_pairs)


def moved(rows, by):
    zeros = jnp.zeros((abs(by), rows.shape[1]), rows.dtype)
    if by > 0:
        return jnp.concatenate([rows[by:], zeros], axis=0)
    return jnp.concatenate([zeros, rows[:by]], axis=0)


def next_frames(even, odd):
    last = lax.broadcasted_iota(jnp.int32, even.shape, 0) % FR == FR - LAG
    up = moved(even, 1)
    ahead_even = jnp.where(last, moved(odd, 1 - FR), up)
    ahead_odd = jnp.where(last, up, moved(odd, 1))
    return jnp.concatenate([ahead_even, ahead_odd], axis=0)


def covariance_kernel(
    row_count,
    counts_ref,
    features_ref,
    mean_now_ref,
    mean_lag_ref,
    cov_now_ref,
    cov_lag_ref,
    weights_ref,
    left_ref,
):
    step = pl.program_id(0)
    _, _, frames, width = features_ref.shape

    def widened(rows):
        return jnp.concatenate([rows] * (width // 128), axis=1)

    def frames_of(j):
        even = features_ref[0, j]
        odd = features_ref[1, j]
        return jnp.concatenate([even, odd], axis=0), next_frames(even, odd)

    def pair_count():
        return jnp.sum(weights_ref[...], axis=0, keepdims=True)

    def mean_of(rows):
        total = jnp.sum(widened(weights_ref[...]) * rows, axis=0, keepdims=True)
        return total / widened(pair_count())

    @pl.when(step == 0)
    def _():
        frame = lax.broadcasted_iota(jnp.int32, (frames, 128), 0)

        def valid_of(core):
            def add_block(b, current):
                return jnp.where(frame // FR == b, counts_ref[CORES * b + core], current)

            current = lax.fori_loop(
                0, frames // FR, add_block, jnp.zeros((frames, 128), jnp.int32)
            )
            return jnp.where(frame % FR < current, 1.0, 0.0)

        even = valid_of(0)
        odd = valid_of(1)
        weights_ref[...] = jnp.concatenate([even, odd], axis=0) * next_frames(even, odd)
        start = lax.axis_index("tm") * row_count
        features, _unused = frames_of(start // width)
        early = (features - mean_of(features)).astype(jnp.bfloat16).astype(jnp.float32)
        left = early * widened(weights_ref[...])
        left_ref[...] = jnp.transpose(left).astype(jnp.bfloat16)

    features, ahead = frames_of(step)
    mean_now = mean_of(features)
    mean_lag = mean_of(ahead)
    mean_now_ref[...] = mean_now
    mean_lag_ref[...] = mean_lag
    early = (features - mean_now).astype(jnp.bfloat16)
    late = (ahead - mean_lag).astype(jnp.bfloat16)
    if row_count == width:
        left = left_ref[...]
    else:
        offset = lax.rem(lax.axis_index("tm") * row_count, width)
        left = left_ref[pl.ds(pl.multiple_of(offset, row_count), row_count), :]
    factor = widened(1.0 / pair_count())
    cov_now_ref[...] = jnp.dot(left, early, preferred_element_type=jnp.float32) * factor
    cov_lag_ref[...] = jnp.dot(left, late, preferred_element_type=jnp.float32) * factor


def covariances(features, frame_counts, row_count):
    _, chunks, frames, chunk = features.shape
    width = chunks * chunk
    row = jax.ShapeDtypeStruct((1, width), jnp.float32)
    matrix = jax.ShapeDtypeStruct((row_count, width), jnp.float32)
    return pl.pallas_call(
        functools.partial(covariance_kernel, row_count),
        out_shape=(row, row, matrix, matrix),
        grid=(chunks,),
        in_specs=[
            pl.BlockSpec(memory_space=pltpu.SMEM),
            pl.BlockSpec(
                features.shape, lambda i: (0, 0, 0, 0), pipeline_mode=pl.Buffered(1)
            ),
        ],
        out_specs=(
            pl.BlockSpec((1, chunk), lambda i: (0, i)),
            pl.BlockSpec((1, chunk), lambda i: (0, i)),
            pl.BlockSpec((row_count, chunk), lambda i: (0, i)),
            pl.BlockSpec((row_count, chunk), lambda i: (0, i)),
        ),
        scratch_shapes=[
            pltpu.VMEM((CORES * frames, 128), jnp.float32),
            pltpu.VMEM((chunk, CORES * frames), jnp.bfloat16),
        ],
        compiler_params=pltpu.CompilerParams(vmem_limit_bytes=60 * 1024 * 1024),
        name="covariances",
    )(frame_counts, features)


def body(positions, atom_pairs, frame_counts):
    devices = lax.axis_size("tm")
    width = atom_pairs.shape[1]
    row_count = width // devices
    chunk = 512 if devices <= 32 else 128
    features = shared_features(
        jnp.transpose(positions, (1, 0, 2)), atom_pairs, devices, chunk
    )
    mean_now, mean_lag, cov_now, cov_lag = covariances(features, frame_counts, row_count)
    return (mean_now.reshape(width), mean_lag.reshape(width), cov_now, cov_lag)


def solution(mesh):
    return jax.shard_map(
        body,
        mesh=mesh,
        in_specs=(P(("groups", "tm"), None, None), P(), P("groups")),
        out_specs=(P("groups"), P("groups"), P(("groups", "tm"), None), P(("groups", "tm"), None)),
        check_vma=False,
    )
```
